32 devices in a mesh: dp: 4 (over y, core), adapter: 8 (over z, x).
Axes of the slice: x: 2, y: 2, z: 4, core: 2. Of those that a mesh axis runs over, the one named last changes fastest.
Arguments:
- activations: bfloat16 [4096, 28672], P('adapter', 'dp'), may hold values from -6 to 6
- cotangent: bfloat16 [4096, 8192], P('adapter', 'dp'), may hold values from -6 to 6
- factor_in: bfloat16 [256, 16, 28672], P('adapter', None, 'dp'), may hold values from -0.03125 to 0.03125
- factor_out: bfloat16 [256, 16, 8192], P('adapter', None, 'dp'), may hold values from -0.0625 to 0.0625
- adapter_ids: int32 [16, 8], P('adapter'), may hold values from 0 to 255, as said below
- router_weights: float32 [16, 8], P('adapter'), may hold values from 0.25 to 1
Outputs:
- input_grad: float32 [4096, 28672], P('adapter', 'dp')
- grad_factor_in: bfloat16 [256, 16, 28672], P('adapter', None, 'dp')
- grad_factor_out: bfloat16 [256, 16, 8192], P('adapter', None, 'dp')
- router_grad: float32 [16, 8], P('adapter')
The draws below stay inside these ranges and needn't reach their ends.
Inputs may be any that keep to these rules, and one draw needn't show every extreme that they name: `adapter_ids`: the 8 adapters of a request are different. The owner of adapter e is e // 32. Requests are taken in aligned groups of 2 (those of one index of adapter); among the 16 adapters named by one group no owner holds more than 2, and in every group some owner holds exactly 2.
All inputs are finite; a program needn't handle non-finite values.
Results may differ from the reference program's by a relative error of at most 0.012.
Values may be sent and summed in bfloat16 or wider, within the bound.
No kernel may reach another device: no remote copies, remote signals or barrier semaphores. Data moves between devices by JAX's collectives and lax.ppermute only.
A program may use at most 128 MiB of HBM per device.

```python
import jax
import jax.numpy as jnp
from jax import lax

D = 8192
FF = 28672
RANK = 16
TOP = 8
REQ_DEV = 2
EXP_DEV = 32
LEN = 256
EXPERTS = 256
REQUESTS = 16
TOKENS = 4096


def draw_adapter_ids(key, part):
    owner_count = EXPERTS // EXP_DEV
    pair_count = REQ_DEV * TOP

    def one_group(group_key):
        keys = jax.random.split(group_key, 4)
        ranked = jax.random.permutation(keys[0], jnp.arange(owner_count, dtype=jnp.int32))
        position = jnp.arange(pair_count, dtype=jnp.int32)
        which = position // 2
        owners = ranked[which]
        base = jax.random.randint(keys[1], (owner_count,), 0, EXP_DEV)
        shifts = jax.random.randint(keys[2], (owner_count,), 1, EXP_DEV)
        local_idx = jnp.where(position % 2 == 0, base[which], (base[which] + shifts[which]) % EXP_DEV)
        chosen = (owners * EXP_DEV + local_idx).astype(jnp.int32)
        order = jax.random.permutation(keys[3], jnp.arange(pair_count, dtype=jnp.int32))
        return chosen[order].reshape(REQ_DEV, TOP).astype(jnp.int32)
    group_keys = jax.random.split(jax.random.fold_in(key, 7), REQUESTS // REQ_DEV)
    return jax.vmap(one_group)(group_keys).reshape(REQUESTS, TOP).astype(jnp.int32)


def levels(rng, dims, cuts, smallest, top_value):
    def one(dim, parts):
        steps = jax.random.uniform(jax.random.fold_in(jax.random.fold_in(rng, 6), dim), (parts,), jnp.float32, smallest / len(cuts), top_value / len(cuts))
        return jnp.repeat(jnp.exp(steps), dims[dim] // parts).reshape((-1,) + (1,) * (len(dims) - dim - 1))

    loudness = one(*cuts[0])
    for cut in cuts[1:]:
        loudness = loudness * one(*cut)
    return loudness


def normal_values(rng, extent, width, most, shards=(), kind=jnp.bfloat16):
    values = jax.random.normal(rng, extent, jnp.float32) * width
    if len(shards) > 0:
        values = levels(rng, extent, shards, -0.22, 0.18) * values
    return jnp.clip(values, min=-most, max=most).astype(kind)


def setup_inputs(seed: int = 0) -> dict:
    key_of = jax.random.split(jax.random.key(seed), 7)
    activations = normal_values(key_of[0], (TOKENS, FF), 1.0, 6.0, ((0, 8), (1, 4)))
    cotangent = normal_values(key_of[1], (TOKENS, D), 1.0, 6.0, ((0, 8), (1, 4)))
    factor_in = normal_values(key_of[2], (EXPERTS, RANK, FF), FF ** -0.5, 0.03125, ((0, 8), (2, 4)))
    factor_out = normal_values(key_of[3], (EXPERTS, RANK, D), D ** -0.5, 0.0625, ((0, 8), (2, 4)))
    adapter_ids = draw_adapter_ids(jax.random.fold_in(key_of[6], 71), 0)
    router_weights = jnp.clip(0.25 + 0.75 * jax.random.uniform(key_of[5], (REQUESTS, TOP), jnp.float32) ** levels(key_of[5], (REQUESTS, TOP), ((0, 8),), -0.2, 0.2), 0.25, 1.0)
    return {"activations": activations, "cotangent": cotangent, "factor_in": factor_in, "factor_out": factor_out, "adapter_ids": adapter_ids, "router_weights": router_weights}


def reference(activations, cotangent, factor_in, factor_out, adapter_ids, router_weights):
    def one_request(item):
        rows_in, rows_out, picks, mixing = item
        inputs32 = rows_in.astype(jnp.float32)
        outputs32 = rows_out.astype(jnp.float32)
        picked_in = factor_in[picks].astype(jnp.float32)
        picked_out = factor_out[picks].astype(jnp.float32)
        projected = jnp.einsum("lf,krf->lkr", inputs32, picked_in)
        pulled = jnp.einsum("ld,krd->lkr", outputs32, picked_out)
        router_row = jnp.sum(projected * pulled, axis=(0, 2))
        pulled_weighted = (mixing[None, :, None] * pulled).astype(jnp.bfloat16)
        projected_weighted = (mixing[None, :, None] * projected).astype(jnp.bfloat16)
        input_rows = jnp.einsum("lkr,krf->lf", pulled_weighted.astype(jnp.float32), picked_in)
        term_in = jnp.einsum("lkr,lf->krf", pulled_weighted.astype(jnp.float32), inputs32).astype(jnp.bfloat16)
        term_out = jnp.einsum("lkr,ld->krd", projected_weighted.astype(jnp.float32), outputs32).astype(jnp.bfloat16)
        return input_rows, term_in, term_out, router_row

    input_rows, term_in, term_out, router_grad = lax.map(
        one_request,
        (activations.reshape(REQUESTS, LEN, FF), cotangent.reshape(REQUESTS, LEN, D), adapter_ids, router_weights))
    flat_ids = adapter_ids.reshape(REQUESTS * TOP)
    grad_factor_in = jax.ops.segment_sum(term_in.reshape(REQUESTS * TOP, RANK, FF).astype(jnp.float32), flat_ids, num_segments=EXPERTS).astype(jnp.bfloat16)
    grad_factor_out = jax.ops.segment_sum(term_out.reshape(REQUESTS * TOP, RANK, D).astype(jnp.float32), flat_ids, num_segments=EXPERTS).astype(jnp.bfloat16)
    input_grad = input_rows.reshape(TOKENS, FF)
    return input_grad, grad_factor_in, grad_factor_out, router_grad
```

```python
import functools
import math

import jax
import jax.numpy as jnp
from jax import lax
from jax.experimental import pallas as pl
from jax.experimental.pallas import tpu as pltpu
from jax.sharding import PartitionSpec as P


CAP = 2
BF = jnp.bfloat16
F32 = jnp.float32
ANY = pl.BlockSpec(memory_space=pl.ANY)
SMEM = pl.BlockSpec(memory_space=pltpu.SMEM)


def swap(x, axis, count, offset):
    return lax.ppermute(x, axis, [(i, i ^ offset) for i in range(count)])


def pick_kernel(groups, me_ref, ids_ref, fin, fout, table_ref, *refs):
    outs = refs[:groups]
    hold, in_sem, out_sem = refs[groups:]
    exp_count, rank, wide = fin.shape
    base = me_ref[0] * exp_count
    loads = []
    for m in range(groups):
        found = jnp.int32(0)
        picks = [jnp.int32(-1)] * CAP
        for b in range(ids_ref.shape[1]):
            for k in range(ids_ref.shape[2]):
                local = ids_ref[m, b, k] - base
                mine = (local >= 0) & (local < exp_count)
                for c in range(CAP):
                    picks[c] = jnp.where(mine & (found == c), local, picks[c])
                found = found + mine.astype(jnp.int32)
        for c in range(CAP):
            table_ref[m, c] = picks[c]
            e = jnp.maximum(picks[c], 0)
            rows = pl.ds(c * rank, rank)
            one = pltpu.make_async_copy(
                fin.at[e], hold.at[m, rows, pl.ds(0, wide)], in_sem.at[m, c, 0]
            )
            two = pltpu.make_async_copy(
                fout.at[e], hold.at[m, rows, pl.ds(wide, fout.shape[2])], in_sem.at[m, c, 1]
            )
            one.start()
            two.start()
            loads.append((one, two))
    stores = []
    for m in range(groups):
        for c in range(CAP):
            for load in loads[m * CAP + c]:
                load.wait()
        store = pltpu.make_async_copy(hold.at[m], outs[m], out_sem.at[m])
        store.start()
        stores.append(store)
    for store in stores:
        store.wait()


def project_kernel(groups, in_tiles, tiles, mask_ref, x_ref, g_ref, *refs):
    pieces = refs[:groups]
    out_ref, rows, total = refs[groups:]
    i = pl.program_id(0)
    rank = pieces[0].shape[0]
    for d in range(groups):
        rows[pl.ds(d * rank, rank), :] = pieces[d][...]
    dims = (((1,), (1,)), ((), ()))

    def add(side, data_ref, first):
        part = lax.dot_general(data_ref[...], rows[...], dims, preferred_element_type=F32)

        @pl.when(first)
        def _():
            total[side] = part

        @pl.when(jnp.logical_not(first))
        def _():
            total[side] += part

    @pl.when(i < in_tiles)
    def _():
        add(0, x_ref, i == 0)

    @pl.when(i >= in_tiles)
    def _():
        add(1, g_ref, i == in_tiles)

    @pl.when(i == tiles - 1)
    def _():
        length = out_ref.shape[1]
        for side in range(2):
            acc = jnp.zeros(out_ref.shape[1:], F32)
            for b in range(mask_ref.shape[0]):
                part = total[side, pl.ds(b * length, length), :]
                acc = jnp.where(mask_ref[b : b + 1, :] > 0, part, acc)
            out_ref[side] = acc


def term_kernel(groups, in_tiles, sums_ref, weight_ref, x_ref, g_ref, *refs):
    outs = refs[:groups]
    weighted_ref, pulled, projected = refs[groups:]
    i = pl.program_id(0)
    rank = outs[0].shape[0]

    @pl.when(i == 0)
    def _():
        length = sums_ref.shape[1]
        for b in range(weight_ref.shape[0]):
            w = weight_ref[b : b + 1, :]
            span = pl.ds(b * length, length)
            part = sums_ref[1] * w
            weighted_ref[span, :] = part.astype(BF)
            pulled[:, span] = part.T.astype(BF)
            projected[:, span] = (sums_ref[0] * w).T.astype(BF)

    @pl.when(i < in_tiles)
    def _():
        part = jnp.dot(pulled[...], x_ref[...], preferred_element_type=F32).astype(BF)
        for d in range(groups):
            outs[d][...] = part[d * rank : (d + 1) * rank]

    @pl.when(i >= in_tiles)
    def _():
        part = jnp.dot(projected[...], g_ref[...], preferred_element_type=F32).astype(BF)
        for d in range(groups):
            outs[d][...] = part[d * rank : (d + 1) * rank]


def input_kernel(chunks, count, *refs):
    weighted = refs[:chunks]
    pieces = refs[chunks : chunks + count]
    out_ref, rows, left = refs[chunks + count :]
    rank = pieces[0].shape[0]
    half = weighted[0].shape[1]

    @pl.when(pl.program_id(0) == 0)
    def _():
        for c in range(chunks):
            left[:, pl.ds(c * half, half)] = weighted[c][...]

    for m in range(count):
        rows[pl.ds(m * rank, rank), :] = pieces[m][...]
    out_ref[...] = jnp.dot(left[...], rows[...], preferred_element_type=F32)


def place(refs, m, rank):
    return refs[m // CAP].at[pl.ds((m % CAP) * rank, rank), :]


def collect_kernel(count, table_ref, *refs):
    pieces = refs[: count // CAP]
    in_ref, out_ref, total = refs[count // CAP :]
    block, rank, wide = in_ref.shape
    for s in range(block):
        e = pl.program_id(0) * block + s
        total[...] = jnp.zeros_like(total)
        for m in range(count):

            @pl.when(table_ref[m] == e)
            def _():
                total[...] += place(pieces, m, rank)[...].astype(F32)

        in_ref[s] = total[:, :wide].astype(BF)
        out_ref[s] = total[:, wide:].astype(BF)


def finish_kernel(late, early, late_ref, early_ref, *refs):
    a, b = late // CAP, early // CAP
    late_hbm, early_hbm = refs[:a], refs[a : a + b]
    in_hbm, out_hbm, held, kept, stage, total, held_sem, kept_sem, out_sem = refs[a + b + 2 :]
    rank, full = total.shape
    wide = in_hbm.shape[2]

    def used(m):
        hit = late_ref[0] == early_ref[m]
        for s in range(1, late):
            hit = hit | (late_ref[s] == early_ref[m])
        return hit & (early_ref[m] >= 0)

    def first(s):
        fresh = late_ref[s] >= 0
        for r in range(s):
            fresh = fresh & (late_ref[r] != late_ref[s])
        return fresh

    def load_late(j):
        return pltpu.make_async_copy(late_hbm[j], held.at[j], held_sem.at[j])

    def load_early(m):
        return pltpu.make_async_copy(place(early_hbm, m, rank), kept.at[m], kept_sem.at[m])

    def stores(s):
        e = jnp.maximum(late_ref[s], 0)
        return (
            pltpu.make_async_copy(stage.at[s, :, pl.ds(0, wide)], in_hbm.at[e], out_sem.at[s, 0]),
            pltpu.make_async_copy(
                stage.at[s, :, pl.ds(wide, full - wide)], out_hbm.at[e], out_sem.at[s, 1]
            ),
        )

    for j in range(a):
        load_late(j).start()
    for m in range(early):

        @pl.when(used(m))
        def _():
            load_early(m).start()

    for j in range(a):
        load_late(j).wait()
    for s in range(late):

        @pl.when(first(s))
        def _():
            total[...] = held[s // CAP, pl.ds((s % CAP) * rank, rank), :].astype(F32)
            for r in range(s + 1, late):

                @pl.when(late_ref[r] == late_ref[s])
                def _():
                    total[...] += held[r // CAP, pl.ds((r % CAP) * rank, rank), :].astype(F32)

            for m in range(early):

                @pl.when(late_ref[s] == early_ref[m])
                def _():
                    load_early(m).wait()
                    total[...] += kept[m].astype(F32)

            stage[s] = total[...].astype(BF)
            for store in stores(s):
                store.start()

    for s in range(late):

        @pl.when(first(s))
        def _():
            for store in stores(s):
                store.wait()


def body(activations, cotangent, factor_in, factor_out, adapter_ids, router_weights):
    groups = lax.axis_size("adapter")
    dp = lax.axis_size("dp")
    me = lax.axis_index("adapter")
    exp_count, rank, wide = factor_in.shape
    narrow = factor_out.shape[2]
    req_count, top_count = adapter_ids.shape
    pair_count = req_count * top_count
    tokens = activations.shape[0]
    length = tokens // req_count
    full = wide + narrow
    tile = math.gcd(wide, narrow)
    in_tiles, tiles = wide // tile, full // tile
    me_arr = me.astype(jnp.int32).reshape(1)
    both = CAP * rank
    piece = jax.ShapeDtypeStruct((both, full), BF)

    def pick(lists):
        count = lists.shape[0]
        return pl.pallas_call(
            functools.partial(pick_kernel, count),
            out_shape=[jax.ShapeDtypeStruct((count, CAP), jnp.int32)] + [piece] * count,
            in_specs=[SMEM, SMEM, ANY, ANY],
            out_specs=[SMEM] + [ANY] * count,
            scratch_shapes=[
                pltpu.VMEM((count, both, full), BF),
                pltpu.SemaphoreType.DMA((count, CAP, 2)),
                pltpu.SemaphoreType.DMA((count,)),
            ],
        )(me_arr, lists, factor_in, factor_out)

    steps = [groups >> (i + 1) for i in range(groups.bit_length() - 1)]
    lists, known = adapter_ids[None], [0]
    slot_table, sent, got = {}, {}, {}
    arrivals = []
    for step in steps:
        fresh = swap(lists, "adapter", groups, step)
        arrivals.append(([d ^ step for d in known], fresh))
        lists = jnp.concatenate([lists, fresh], axis=0)
        known = known + [d ^ step for d in known]
    arrivals.append(([0], adapter_ids[None]))
    for which, fresh in arrivals:
        picked = pick(fresh)
        for m, d in enumerate(which):
            slot_table[d] = picked[0][m]
            sent[d] = picked[1 + m]
    last = steps[-1]
    chunks = [
        [d for d in known if not d & last],
        [d for d in known if d & last],
    ]
    chunks = [sorted(c, key=lambda d: (d >= groups // 2, d)) for c in chunks]
    for chunk in chunks:
        for d in chunk:
            got[d] = sent[d] if d == 0 else swap(sent[d], "adapter", groups, d)

    my_pairs = adapter_ids.reshape(pair_count)
    my_owner = my_pairs // exp_count
    order = jnp.arange(pair_count)
    before = order[:, None] > order[None, :]
    my_slot = jnp.sum((my_owner[:, None] == my_owner[None, :]) & before, axis=1)
    far = jnp.array([d for c in chunks for d in c], jnp.int32) ^ me
    chosen = (
        (my_owner[None, None, :] == far[:, None, None])
        & (my_slot[None, None, :] == jnp.arange(CAP)[None, :, None])
    ).astype(F32)
    by_request = chosen.reshape(groups * CAP, req_count, top_count)
    mask = jnp.repeat(jnp.sum(by_request, axis=2).T, rank, axis=1)
    weight = jnp.repeat(jnp.sum(by_request * router_weights[None], axis=2).T, rank, axis=1)

    rows = len(chunks[0]) * both
    x_spec = pl.BlockSpec((tokens, tile), lambda i: (0, jnp.minimum(i, in_tiles - 1)))
    g_spec = pl.BlockSpec((tokens, tile), lambda i: (0, jnp.maximum(i - in_tiles, 0)))
    piece_spec = pl.BlockSpec((both, tile), lambda i: (0, i))
    small = pl.BlockSpec((req_count, rows), lambda i: (0, 0))
    sums_spec = pl.BlockSpec((2, length, rows), lambda i: (0, 0, 0))
    weighted_spec = pl.BlockSpec((tokens, rows), lambda i: (0, 0))

    back, weighted, sums = {}, [], []
    for n, chunk in enumerate(chunks):
        count = len(chunk)
        my_mask = mask[:, n * rows : (n + 1) * rows]
        if n:
            my_mask, weighted[-1] = lax.optimization_barrier((my_mask, weighted[-1]))
        part = pl.pallas_call(
            functools.partial(project_kernel, count, in_tiles, tiles),
            out_shape=jax.ShapeDtypeStruct((2, length, rows), F32),
            grid=(tiles,),
            in_specs=[small, x_spec, g_spec] + [piece_spec] * count,
            out_specs=sums_spec,
            scratch_shapes=[pltpu.VMEM((rows, tile), BF), pltpu.VMEM((2, tokens, rows), F32)],
        )(my_mask, activations, cotangent, *[got[d] for d in chunk])
        step = 1
        while step < dp:
            part = part + swap(part, "dp", dp, step)
            step *= 2
        done = pl.pallas_call(
            functools.partial(term_kernel, count, in_tiles),
            out_shape=[piece] * count + [jax.ShapeDtypeStruct((tokens, rows), BF)],
            grid=(tiles,),
            in_specs=[sums_spec, small, x_spec, g_spec],
            out_specs=[piece_spec] * count + [weighted_spec],
            scratch_shapes=[pltpu.VMEM((rows, tokens), BF)] * 2,
        )(part, weight[:, n * rows : (n + 1) * rows], activations, cotangent)
        sums.append(part)
        weighted.append(done[-1])
        for m, d in enumerate(chunk):
            back[d] = done[m] if d == 0 else swap(done[m], "adapter", groups, d)

    everything = [d for c in chunks for d in c]
    input_grad = pl.pallas_call(
        functools.partial(input_kernel, len(chunks), groups),
        out_shape=jax.ShapeDtypeStruct((tokens, wide), F32),
        grid=(in_tiles,),
        in_specs=[weighted_spec] * len(chunks) + [piece_spec] * groups,
        out_specs=pl.BlockSpec((tokens, tile), lambda i: (0, i)),
        scratch_shapes=[
            pltpu.VMEM((groups * both, tile), BF),
            pltpu.VMEM((tokens, len(chunks) * rows), BF),
        ],
        name="input",
    )(*weighted, *[got[d] for d in everything])

    per_slot = jnp.concatenate([jnp.sum(s[0] * s[1], axis=0) for s in sums])
    per_slot = jnp.sum(per_slot.reshape(groups * CAP, rank), axis=1)
    router_grad = jnp.sum(by_request * per_slot[:, None, None], axis=0)

    tables = [jnp.concatenate([slot_table[d] for d in c]) for c in chunks]
    early, late = len(chunks[0]) * CAP, len(chunks[1]) * CAP
    block = math.gcd(exp_count, 4)
    grads = [
        jax.ShapeDtypeStruct(factor_in.shape, BF),
        jax.ShapeDtypeStruct(factor_out.shape, BF),
    ]
    grads = pl.pallas_call(
        functools.partial(collect_kernel, early),
        out_shape=grads,
        grid=(exp_count // block,),
        in_specs=[SMEM] + [pl.BlockSpec(memory_space=pltpu.VMEM)] * len(chunks[0]),
        out_specs=[
            pl.BlockSpec((block, rank, wide), lambda i: (i, 0, 0)),
            pl.BlockSpec((block, rank, narrow), lambda i: (i, 0, 0)),
        ],
        scratch_shapes=[pltpu.VMEM((rank, full), F32)],
        name="collect",
    )(tables[0], *[back[d] for d in chunks[0]])
    grad_factor_in, grad_factor_out = pl.pallas_call(
        functools.partial(finish_kernel, late, early),
        out_shape=[jax.ShapeDtypeStruct(g.shape, BF) for g in grads],
        in_specs=[SMEM] * 2 + [ANY] * (groups + 2),
        out_specs=[ANY] * 2,
        scratch_shapes=[
            pltpu.VMEM((len(chunks[1]), both, full), BF),
            pltpu.VMEM((early, rank, full), BF),
            pltpu.VMEM((late, rank, full), BF),
            pltpu.VMEM((rank, full), F32),
            pltpu.SemaphoreType.DMA((len(chunks[1]),)),
            pltpu.SemaphoreType.DMA((early,)),
            pltpu.SemaphoreType.DMA((late, 2)),
        ],
        input_output_aliases={groups + 2: 0, groups + 3: 1},
        name="finish",
    )(tables[1], tables[0], *[back[d] for d in chunks[1]], *[back[d] for d in chunks[0]], *grads)
    return (input_grad, grad_factor_in, grad_factor_out, router_grad)


def solution(mesh):
    return jax.shard_map(
        body,
        mesh=mesh,
        in_specs=(
            P("adapter", "dp"),
            P("adapter", "dp"),
            P("adapter", None, "dp"),
            P("adapter", None, "dp"),
            P("adapter", None),
            P("adapter", None),
        ),
        out_specs=(
            P("adapter", "dp"),
            P("adapter", None, "dp"),
            P("adapter", None, "dp"),
            P("adapter", None),
        ),
        check_vma=False,
    )
```

```python
import functools
import math

import jax
import jax.numpy as jnp
from jax import lax
from jax.experimental import pallas as pl
from jax.experimental.pallas import tpu as pltpu
from jax.sharding import PartitionSpec as P


CAP = 2
BF = jnp.bfloat16
F32 = jnp.float32
ANY = pl.BlockSpec(memory_space=pl.ANY)
SMEM = pl.BlockSpec(memory_space=pltpu.SMEM)
VMEM = pl.BlockSpec(memory_space=pltpu.VMEM)
HBM = pl.BlockSpec(memory_space=pltpu.HBM)


def plan(groups):
    steps = [groups >> (i + 1) for i in range(groups.bit_length() - 1)]
    half, last = groups // 2, steps[-1]
    if groups > 4:
        steps[0] += half // 2
    out = []
    for part in (0, last):
        near = [d for d in range(half) if d & last == part]
        far = [d for d in range(half, groups) if d & last == part]
        out.append(near + far)
    home = [list(part) for part in out]
    return steps, out, home


def swap(x, axis, count, offset):
    return lax.ppermute(x, axis, [(i, i ^ offset) for i in range(count)])


def pick_kernel(groups, me_ref, ids_ref, fin, fout, table_ref, *refs):
    outs = refs[:groups]
    (in_sem,) = refs[groups:]
    exp_count, rank, wide = fin.shape
    base = me_ref[0] * exp_count
    loads = []
    for m in range(groups):
        found = jnp.int32(0)
        picks = [jnp.int32(-1)] * CAP
        for b in range(ids_ref.shape[1]):
            for k in range(ids_ref.shape[2]):
                local = ids_ref[m, b, k] - base
                mine = (local >= 0) & (local < exp_count)
                for c in range(CAP):
                    picks[c] = jnp.where(mine & (found == c), local, picks[c])
                found = found + mine.astype(jnp.int32)
        for c in range(CAP):
            table_ref[m, c] = picks[c]
            e = jnp.maximum(picks[c], 0)
            rows = pl.ds(c * rank, rank)
            one = pltpu.make_async_copy(
                fin.at[e], outs[m].at[rows, pl.ds(0, wide)], in_sem.at[m, c, 0]
            )
            two = pltpu.make_async_copy(
                fout.at[e], outs[m].at[rows, pl.ds(wide, fout.shape[2])], in_sem.at[m, c, 1]
            )
            one.start()
            two.start()
            loads.append((one, two))
    for pair in loads:
        for load in pair:
            load.wait()


def project_kernel(groups, in_tiles, tiles, mask_ref, x_ref, g_ref, *refs):
    pieces = refs[:groups]
    out_ref, rows, total = refs[groups:]
    i = pl.program_id(0)
    rank = pieces[0].shape[0]
    for d in range(groups):
        rows[pl.ds(d * rank, rank), :] = pieces[d][...]
    dims = (((1,), (1,)), ((), ()))

    def add(side, data_ref, first):
        part = lax.dot_general(data_ref[...], rows[...], dims, preferred_element_type=F32)

        @pl.when(first)
        def _():
            total[side] = part

        @pl.when(jnp.logical_not(first))
        def _():
            total[side] += part

    @pl.when(i < in_tiles)
    def _():
        add(0, x_ref, i == 0)

    @pl.when(i >= in_tiles)
    def _():
        add(1, g_ref, i == in_tiles)

    @pl.when(i == tiles - 1)
    def _():
        length = out_ref.shape[1]
        for side in range(2):
            acc = jnp.zeros(out_ref.shape[1:], F32)
            for b in range(mask_ref.shape[0]):
                part = total[side, pl.ds(b * length, length), :]
                acc = jnp.where(mask_ref[b : b + 1, :] > 0, part, acc)
            out_ref[side] = acc


def term_kernel(groups, in_tiles, sums_ref, weight_ref, x_ref, g_ref, *refs):
    outs = refs[:groups]
    weighted_ref, pulled, projected = refs[groups:]
    i = pl.program_id(0)
    rank = outs[0].shape[0]

    @pl.when(i == 0)
    def _():
        length = sums_ref.shape[1]
        for b in range(weight_ref.shape[0]):
            w = weight_ref[b : b + 1, :]
            span = pl.ds(b * length, length)
            part = sums_ref[1] * w
            weighted_ref[span, :] = part.astype(BF)
            pulled[:, span] = part.T.astype(BF)
            projected[:, span] = (sums_ref[0] * w).T.astype(BF)

    @pl.when(i < in_tiles)
    def _():
        part = jnp.dot(pulled[...], x_ref[...], preferred_element_type=F32).astype(BF)
        for d in range(groups):
            outs[d][...] = part[d * rank : (d + 1) * rank]

    @pl.when(i >= in_tiles)
    def _():
        part = jnp.dot(projected[...], g_ref[...], preferred_element_type=F32).astype(BF)
        for d in range(groups):
            outs[d][...] = part[d * rank : (d + 1) * rank]


def input_kernel(chunks, count, *refs):
    weighted = refs[:chunks]
    pieces = refs[chunks : chunks + count]
    out_ref, rows, left = refs[chunks + count :]
    rank = pieces[0].shape[0]
    half = weighted[0].shape[1]

    @pl.when(pl.program_id(0) == 0)
    def _():
        for c in range(chunks):
            left[:, pl.ds(c * half, half)] = weighted[c][...]

    for m in range(count):
        rows[pl.ds(m * rank, rank), :] = pieces[m][...]
    out_ref[...] = jnp.dot(left[...], rows[...], preferred_element_type=F32)


def place(refs, m, rank):
    return refs[m // CAP].at[pl.ds((m % CAP) * rank, rank), :]


def collect_kernel(count, table_ref, *refs):
    pieces = refs[: count // CAP]
    in_ref, out_ref, total = refs[count // CAP :]
    block, rank, wide = in_ref.shape
    for s in range(block):
        e = pl.program_id(0) * block + s
        total[...] = jnp.zeros_like(total)
        for m in range(count):

            @pl.when(table_ref[m] == e)
            def _():
                total[...] += place(pieces, m, rank)[...].astype(F32)

        in_ref[s] = total[:, :wide].astype(BF)
        out_ref[s] = total[:, wide:].astype(BF)


def finish_kernel(late, early, late_ref, early_ref, *refs):
    a, b = late // CAP, early // CAP
    late_refs, early_hbm = refs[:a], refs[a : a + b]
    in_hbm, out_hbm, kept, stage, total, kept_sem, out_sem = refs[a + b + 2 :]
    rank, full = total.shape
    wide = in_hbm.shape[2]

    def used(m):
        hit = late_ref[0] == early_ref[m]
        for s in range(1, late):
            hit = hit | (late_ref[s] == early_ref[m])
        return hit & (early_ref[m] >= 0)

    def first(s):
        fresh = late_ref[s] >= 0
        for r in range(s):
            fresh = fresh & (late_ref[r] != late_ref[s])
        return fresh

    def load_early(m):
        return pltpu.make_async_copy(place(early_hbm, m, rank), kept.at[m], kept_sem.at[m])

    def stores(s):
        e = jnp.maximum(late_ref[s], 0)
        return (
            pltpu.make_async_copy(stage.at[s, :, pl.ds(0, wide)], in_hbm.at[e], out_sem.at[s, 0]),
            pltpu.make_async_copy(
                stage.at[s, :, pl.ds(wide, full - wide)], out_hbm.at[e], out_sem.at[s, 1]
            ),
        )

    for m in range(early):

        @pl.when(used(m))
        def _():
            load_early(m).start()

    for s in range(late):

        @pl.when(first(s))
        def _():
            total[...] = place(late_refs, s, rank)[...].astype(F32)
            for r in range(s + 1, late):

                @pl.when(late_ref[r] == late_ref[s])
                def _():
                    total[...] += place(late_refs, r, rank)[...].astype(F32)

            for m in range(early):

                @pl.when(late_ref[s] == early_ref[m])
                def _():
                    load_early(m).wait()
                    total[...] += kept[m].astype(F32)

            stage[s] = total[...].astype(BF)
            for store in stores(s):
                store.start()

    for s in range(late):

        @pl.when(first(s))
        def _():
            for store in stores(s):
                store.wait()


def body(activations, cotangent, factor_in, factor_out, adapter_ids, router_weights):
    groups = lax.axis_size("adapter")
    dp = lax.axis_size("dp")
    me = lax.axis_index("adapter")
    exp_count, rank, wide = factor_in.shape
    narrow = factor_out.shape[2]
    req_count, top_count = adapter_ids.shape
    pair_count = req_count * top_count
    tokens = activations.shape[0]
    length = tokens // req_count
    full = wide + narrow
    tile = math.gcd(wide, narrow)
    in_tiles, tiles = wide // tile, full // tile
    me_arr = me.astype(jnp.int32).reshape(1)
    both = CAP * rank
    piece = jax.ShapeDtypeStruct((both, full), BF)

    def pick(lists, fast):
        count = lists.shape[0]
        return pl.pallas_call(
            functools.partial(pick_kernel, count),
            out_shape=[jax.ShapeDtypeStruct((count, CAP), jnp.int32)]
            + [pltpu.VMEM((both, full), BF) if fast else piece] * count,
            in_specs=[SMEM, SMEM, HBM, HBM],
            out_specs=[SMEM] + [VMEM] * count,
            scratch_shapes=[pltpu.SemaphoreType.DMA((count, CAP, 2))],
        )(me_arr, lists, factor_in, factor_out)

    steps, chunks, homes = plan(groups)
    lists, known = adapter_ids[None], [0]
    slot_table, sent, got = {}, {}, {}
    arrivals = []
    for step in steps:
        fresh = swap(lists, "adapter", groups, step)
        arrivals.append(([d ^ step for d in known], fresh))
        lists = jnp.concatenate([lists, fresh], axis=0)
        known = known + [d ^ step for d in known]
    arrivals.append(([0], adapter_ids[None]))
    for n, (which, fresh) in enumerate(arrivals):
        picked = pick(fresh, n == 0)
        for m, d in enumerate(which):
            slot_table[d] = picked[0][m]
            sent[d] = picked[1 + m]
    for chunk in chunks:
        for d in chunk:
            got[d] = sent[d] if d == 0 else swap(sent[d], "adapter", groups, d)

    my_pairs = adapter_ids.reshape(pair_count)
    my_owner = my_pairs // exp_count
    order = jnp.arange(pair_count)
    before = order[:, None] > order[None, :]
    my_slot = jnp.sum((my_owner[:, None] == my_owner[None, :]) & before, axis=1)
    far = jnp.array([d for c in chunks for d in c], jnp.int32) ^ me
    chosen = (
        (my_owner[None, None, :] == far[:, None, None])
        & (my_slot[None, None, :] == jnp.arange(CAP)[None, :, None])
    ).astype(F32)
    by_request = chosen.reshape(groups * CAP, req_count, top_count)
    mask = jnp.repeat(jnp.sum(by_request, axis=2).T, rank, axis=1)
    weight = jnp.repeat(jnp.sum(by_request * router_weights[None], axis=2).T, rank, axis=1)

    rows = len(chunks[0]) * both
    x_spec = pl.BlockSpec((tokens, tile), lambda i: (0, jnp.minimum(i, in_tiles - 1)))
    g_spec = pl.BlockSpec((tokens, tile), lambda i: (0, jnp.maximum(i - in_tiles, 0)))
    piece_spec = pl.BlockSpec((both, tile), lambda i: (0, i))
    small = pl.BlockSpec((req_count, rows), lambda i: (0, 0))
    sums_spec = pl.BlockSpec((2, length, rows), lambda i: (0, 0, 0))
    weighted_spec = pl.BlockSpec((tokens, rows), lambda i: (0, 0))

    back, weighted, sums = {}, [], []
    for n, chunk in enumerate(chunks):
        count = len(chunk)
        my_mask = mask[:, n * rows : (n + 1) * rows]
        if n:
            my_mask, weighted[-1] = lax.optimization_barrier((my_mask, weighted[-1]))
        part = pl.pallas_call(
            functools.partial(project_kernel, count, in_tiles, tiles),
            out_shape=jax.ShapeDtypeStruct((2, length, rows), F32),
            grid=(tiles,),
            in_specs=[small, x_spec, g_spec] + [piece_spec] * count,
            out_specs=sums_spec,
            scratch_shapes=[pltpu.VMEM((rows, tile), BF), pltpu.VMEM((2, tokens, rows), F32)],
        )(my_mask, activations, cotangent, *[got[d] for d in chunk])
        step = 1
        while step < dp:
            part = part + swap(part, "dp", dp, step)
            step *= 2
        done = pl.pallas_call(
            functools.partial(term_kernel, count, in_tiles),
            out_shape=[piece] * count + [jax.ShapeDtypeStruct((tokens, rows), BF)],
            grid=(tiles,),
            in_specs=[sums_spec, small, x_spec, g_spec],
            out_specs=[piece_spec] * count + [weighted_spec],
            scratch_shapes=[pltpu.VMEM((rows, tokens), BF)] * 2,
        )(part, weight[:, n * rows : (n + 1) * rows], activations, cotangent)
        sums.append(part)
        weighted.append(done[-1])
        for d in homes[n]:
            mine = done[chunk.index(d)]
            back[d] = mine if d == 0 else swap(mine, "adapter", groups, d)

    everything = [d for c in chunks for d in c]
    input_grad = pl.pallas_call(
        functools.partial(input_kernel, len(chunks), groups),
        out_shape=jax.ShapeDtypeStruct((tokens, wide), F32),
        grid=(in_tiles,),
        in_specs=[weighted_spec] * len(chunks) + [piece_spec] * groups,
        out_specs=pl.BlockSpec((tokens, tile), lambda i: (0, i)),
        scratch_shapes=[
            pltpu.VMEM((groups * both, tile), BF),
            pltpu.VMEM((tokens, len(chunks) * rows), BF),
        ],
        name="input",
    )(*weighted, *[got[d] for d in everything])

    per_slot = jnp.concatenate([jnp.sum(s[0] * s[1], axis=0) for s in sums])
    per_slot = jnp.sum(per_slot.reshape(groups * CAP, rank), axis=1)
    router_grad = jnp.sum(by_request * per_slot[:, None, None], axis=0)

    stages = [homes[0], homes[1][:-1], homes[1][-1:]]
    tables = [jnp.concatenate([slot_table[d] for d in stage]) for stage in stages]
    early = len(stages[0]) * CAP
    block = math.gcd(exp_count, 4)
    grads = pl.pallas_call(
        functools.partial(collect_kernel, early),
        out_shape=[
            jax.ShapeDtypeStruct(factor_in.shape, BF),
            jax.ShapeDtypeStruct(factor_out.shape, BF),
        ],
        grid=(exp_count // block,),
        in_specs=[SMEM] + [VMEM] * len(stages[0]),
        out_specs=[
            pl.BlockSpec((block, rank, wide), lambda i: (i, 0, 0)),
            pl.BlockSpec((block, rank, narrow), lambda i: (i, 0, 0)),
        ],
        scratch_shapes=[pltpu.VMEM((rank, full), F32)],
        name="collect",
    )(tables[0], *[back[d] for d in stages[0]])
    seen, seen_table = list(stages[0]), tables[0]
    for n in (1, 2):
        late, early = len(stages[n]) * CAP, len(seen) * CAP
        arrays = len(stages[n]) + len(seen)
        grads = pl.pallas_call(
            functools.partial(finish_kernel, late, early),
            out_shape=[jax.ShapeDtypeStruct(g.shape, BF) for g in grads],
            in_specs=[SMEM] * 2 + [VMEM] * len(stages[n]) + [ANY] * len(seen) + [HBM] * 2,
            out_specs=[HBM] * 2,
            scratch_shapes=[
                pltpu.VMEM((early, rank, full), BF),
                pltpu.VMEM((late, rank, full), BF),
                pltpu.VMEM((rank, full), F32),
                pltpu.SemaphoreType.DMA((early,)),
                pltpu.SemaphoreType.DMA((late, 2)),
            ],
            input_output_aliases={arrays + 2: 0, arrays + 3: 1},
        )(tables[n], seen_table, *[back[d] for d in stages[n] + seen], *grads)
        seen, seen_table = seen + stages[n], jnp.concatenate([seen_table, tables[n]])
    grad_factor_in, grad_factor_out = grads
    return (input_grad, grad_factor_in, grad_factor_out, router_grad)


def solution(mesh):
    return jax.shard_map(
        body,
        mesh=mesh,
        in_specs=(
            P("adapter", "dp"),
            P("adapter", "dp"),
            P("adapter", None, "dp"),
            P("adapter", None, "dp"),
            P("adapter", None),
            P("adapter", None),
        ),
        out_specs=(
            P("adapter", "dp"),
            P("adapter", None, "dp"),
            P("adapter", None, "dp"),
            P("adapter", None),
        ),
        check_vma=False,
    )
```

```python
import functools
import math

import jax
import jax.numpy as jnp
from jax import lax
from jax.experimental import pallas as pl
from jax.experimental.pallas import tpu as pltpu
from jax.sharding import PartitionSpec as P


CAP = 2
BF = jnp.bfloat16
F32 = jnp.float32
ANY = pl.BlockSpec(memory_space=pl.ANY)
SMEM = pl.BlockSpec(memory_space=pltpu.SMEM)
VMEM = pl.BlockSpec(memory_space=pltpu.VMEM)
HBM = pl.BlockSpec(memory_space=pltpu.HBM)


def plan(groups):
    steps = [groups >> (i + 1) for i in range(groups.bit_length() - 1)]
    half, last = groups // 2, steps[-1]
    if groups > 4:
        steps[0] += half // 2
    out = []
    for part in (0, last):
        near = [d for d in range(half) if d & last == part]
        far = [d for d in range(half, groups) if d & last == part]
        out.append(near + far)
    home = [list(part) for part in out]
    return steps, out, home


def swap(x, axis, count, offset):
    return lax.ppermute(x, axis, [(i, i ^ offset) for i in range(count)])


def pick_kernel(groups, me_ref, ids_ref, fin, fout, table_ref, *refs):
    outs = refs[:groups]
    in_sem, ids, ids_sem = refs[groups:]
    fetch = pltpu.make_async_copy(ids_ref, ids, ids_sem)
    fetch.start()
    fetch.wait()
    exp_count, rank, wide = fin.shape
    base = me_ref[0] * exp_count
    loads = []
    for m in range(groups):
        found = jnp.int32(0)
        picks = [jnp.int32(-1)] * CAP
        for b in range(ids_ref.shape[1]):
            for k in range(ids_ref.shape[2]):
                local = ids[m, b, k] - base
                mine = (local >= 0) & (local < exp_count)
                for c in range(CAP):
                    picks[c] = jnp.where(mine & (found == c), local, picks[c])
                found = found + mine.astype(jnp.int32)
        for c in range(CAP):
            table_ref[m, c] = picks[c]
            e = jnp.maximum(picks[c], 0)
            rows = pl.ds(c * rank, rank)
            one = pltpu.make_async_copy(
                fin.at[e], outs[m].at[rows, pl.ds(0, wide)], in_sem.at[m, c, 0]
            )
            two = pltpu.make_async_copy(
                fout.at[e], outs[m].at[rows, pl.ds(wide, fout.shape[2])], in_sem.at[m, c, 1]
            )
            one.start()
            two.start()
            loads.append((one, two))
    for pair in loads:
        for load in pair:
            load.wait()


def project_kernel(groups, in_tiles, tiles, mask_ref, x_ref, g_ref, *refs):
    pieces = refs[:groups]
    out_ref, rows, total = refs[groups:]
    i = pl.program_id(0)
    rank = pieces[0].shape[0]
    for d in range(groups):
        rows[pl.ds(d * rank, rank), :] = pieces[d][...]
    dims = (((1,), (1,)), ((), ()))

    def add(side, data_ref, first):
        part = lax.dot_general(data_ref[...], rows[...], dims, preferred_element_type=F32)

        @pl.when(first)
        def _():
            total[side] = part

        @pl.when(jnp.logical_not(first))
        def _():
            total[side] += part

    @pl.when(i < in_tiles)
    def _():
        add(0, x_ref, i == 0)

    @pl.when(i >= in_tiles)
    def _():
        add(1, g_ref, i == in_tiles)

    @pl.when(i == tiles - 1)
    def _():
        length = out_ref.shape[1]
        for side in range(2):
            acc = jnp.zeros(out_ref.shape[1:], F32)
            for b in range(mask_ref.shape[0]):
                part = total[side, pl.ds(b * length, length), :]
                acc = jnp.where(mask_ref[b : b + 1, :] > 0, part, acc)
            out_ref[side] = acc


def term_kernel(groups, in_tiles, sums_ref, weight_ref, x_ref, g_ref, *refs):
    outs = refs[:groups]
    weighted_ref, pulled, projected = refs[groups:]
    i = pl.program_id(0)
    rank = outs[0].shape[0]

    @pl.when(i == 0)
    def _():
        length = sums_ref.shape[1]
        for b in range(weight_ref.shape[0]):
            w = weight_ref[b : b + 1, :]
            span = pl.ds(b * length, length)
            part = sums_ref[1] * w
            weighted_ref[span, :] = part.astype(BF)
            pulled[:, span] = part.T.astype(BF)
            projected[:, span] = (sums_ref[0] * w).T.astype(BF)

    @pl.when(i < in_tiles)
    def _():
        part = jnp.dot(pulled[...], x_ref[...], preferred_element_type=F32).astype(BF)
        for d in range(groups):
            outs[d][...] = part[d * rank : (d + 1) * rank]

    @pl.when(i >= in_tiles)
    def _():
        part = jnp.dot(projected[...], g_ref[...], preferred_element_type=F32).astype(BF)
        for d in range(groups):
            outs[d][...] = part[d * rank : (d + 1) * rank]


def input_kernel(chunks, count, *refs):
    weighted = refs[:chunks]
    pieces = refs[chunks : chunks + count]
    out_ref, rows, left = refs[chunks + count :]
    rank = pieces[0].shape[0]
    half = weighted[0].shape[1]

    @pl.when(pl.program_id(0) == 0)
    def _():
        for c in range(chunks):
            left[:, pl.ds(c * half, half)] = weighted[c][...]

    for m in range(count):
        rows[pl.ds(m * rank, rank), :] = pieces[m][...]
    out_ref[...] = jnp.dot(left[...], rows[...], preferred_element_type=F32)


def place(refs, m, rank):
    return refs[m // CAP].at[pl.ds((m % CAP) * rank, rank), :]


def collect_kernel(count, table_ref, *refs):
    pieces = refs[: count // CAP]
    in_ref, out_ref, total = refs[count // CAP :]
    block, rank, wide = in_ref.shape
    for s in range(block):
        e = pl.program_id(0) * block + s
        total[...] = jnp.zeros_like(total)
        for m in range(count):

            @pl.when(table_ref[m] == e)
            def _():
                total[...] += place(pieces, m, rank)[...].astype(F32)

        in_ref[s] = total[:, :wide].astype(BF)
        out_ref[s] = total[:, wide:].astype(BF)


def fresh(table_ref, s):
    new = table_ref[s] >= 0
    for r in range(s):
        new = new & (table_ref[r] != table_ref[s])
    return new


def stores(table_ref, s, stage, in_hbm, out_hbm, out_sem):
    e = jnp.maximum(table_ref[s], 0)
    wide, narrow = in_hbm.shape[2], out_hbm.shape[2]
    return (
        pltpu.make_async_copy(stage.at[s, :, pl.ds(0, wide)], in_hbm.at[e], out_sem.at[s, 0]),
        pltpu.make_async_copy(stage.at[s, :, pl.ds(wide, narrow)], out_hbm.at[e], out_sem.at[s, 1]),
    )


def finish_kernel(late, early, ends, late_ref, early_ref, end_ref, *refs):
    a, b = late // CAP, early // CAP
    late_refs, early_hbm = refs[:a], refs[a : a + b]
    in_hbm, out_hbm, ahead, kept, stage, total, kept_sem, out_sem = refs[a + b + 2 :]
    rank, _ = total.shape

    def load_early(m):
        return pltpu.make_async_copy(place(early_hbm, m, rank), kept.at[m], kept_sem.at[m])

    def used(m):
        hit = late_ref[0] == early_ref[m]
        for s in range(1, late):
            hit = hit | (late_ref[s] == early_ref[m])
        for s in range(ends):
            hit = hit | (end_ref[s] == early_ref[m])
        return hit & (early_ref[m] >= 0)

    def add(e, known, known_ref, terms):
        for m in range(known):

            @pl.when((known_ref[m] == e) & (e >= 0))
            def _():
                total[...] += terms(m)[...].astype(F32)

    for m in range(early):

        @pl.when(used(m))
        def _():
            load_early(m).start()

    for m in range(early):

        @pl.when(used(m))
        def _():
            load_early(m).wait()

    for s in range(late):

        @pl.when(fresh(late_ref, s))
        def _():
            total[...] = jnp.zeros_like(total)
            add(late_ref[s], late, late_ref, lambda m: place(late_refs, m, rank))
            add(late_ref[s], early, early_ref, lambda m: kept.at[m])
            stage[s] = total[...].astype(BF)
            for store in stores(late_ref, s, stage, in_hbm, out_hbm, out_sem):
                store.start()

    for s in range(ends):
        total[...] = jnp.zeros_like(total)
        add(end_ref[s], late, late_ref, lambda m: place(late_refs, m, rank))
        add(end_ref[s], early, early_ref, lambda m: kept.at[m])
        ahead[s] = total[...]

    for s in range(late):

        @pl.when(fresh(late_ref, s))
        def _():
            for store in stores(late_ref, s, stage, in_hbm, out_hbm, out_sem):
                store.wait()


def end_kernel(ends, end_ref, *refs):
    end_refs, ahead = refs[: ends // CAP], refs[ends // CAP]
    in_hbm, out_hbm, stage, out_sem = refs[ends // CAP + 3 :]
    rank = stage.shape[1]
    for s in range(ends):

        @pl.when(fresh(end_ref, s))
        def _():
            stage[s] = (place(end_refs, s, rank)[...].astype(F32) + ahead[s]).astype(BF)
            for r in range(s + 1, ends):

                @pl.when(end_ref[r] == end_ref[s])
                def _():
                    total = ahead[s]
                    for m in range(s, ends):
                        same = (end_ref[m] == end_ref[s]).astype(F32)
                        total = total + same * place(end_refs, m, rank)[...].astype(F32)
                    stage[s] = total.astype(BF)

            for store in stores(end_ref, s, stage, in_hbm, out_hbm, out_sem):
                store.start()

    for s in range(ends):

        @pl.when(fresh(end_ref, s))
        def _():
            for store in stores(end_ref, s, stage, in_hbm, out_hbm, out_sem):
                store.wait()


def body(activations, cotangent, factor_in, factor_out, adapter_ids, router_weights):
    groups = lax.axis_size("adapter")
    dp = lax.axis_size("dp")
    me = lax.axis_index("adapter")
    exp_count, rank, wide = factor_in.shape
    narrow = factor_out.shape[2]
    req_count, top_count = adapter_ids.shape
    pair_count = req_count * top_count
    tokens = activations.shape[0]
    length = tokens // req_count
    full = wide + narrow
    tile = math.gcd(wide, narrow)
    in_tiles, tiles = wide // tile, full // tile
    me_arr = me.astype(jnp.int32).reshape(1)
    both = CAP * rank
    piece = jax.ShapeDtypeStruct((both, full), BF)

    def pick(lists, fast):
        count = lists.shape[0]
        return pl.pallas_call(
            functools.partial(pick_kernel, count),
            out_shape=[jax.ShapeDtypeStruct((count, CAP), jnp.int32)]
            + [pltpu.VMEM((both, full), BF) if fast else piece] * count,
            in_specs=[SMEM, VMEM, HBM, HBM],
            out_specs=[SMEM] + [VMEM] * count,
            scratch_shapes=[
                pltpu.SemaphoreType.DMA((count, CAP, 2)),
                pltpu.SMEM(lists.shape, jnp.int32),
                pltpu.SemaphoreType.DMA,
            ],
        )(me_arr, pltpu.with_memory_space_constraint(lists, pltpu.VMEM), factor_in, factor_out)

    steps, chunks, homes = plan(groups)
    lists, known = adapter_ids[None], [0]
    slot_table, sent, got = {}, {}, {}
    arrivals = []
    for step in steps:
        fresh = swap(lists, "adapter", groups, step)
        arrivals.append(([d ^ step for d in known], fresh))
        lists = jnp.concatenate([lists, fresh], axis=0)
        known = known + [d ^ step for d in known]
    arrivals.append(([0], adapter_ids[None]))
    for n, (which, fresh) in enumerate(arrivals):
        picked = pick(fresh, n == 0)
        for m, d in enumerate(which):
            slot_table[d] = picked[0][m]
            sent[d] = picked[1 + m]
    for chunk in chunks:
        for d in chunk:
            got[d] = sent[d] if d == 0 else swap(sent[d], "adapter", groups, d)

    my_pairs = adapter_ids.reshape(pair_count)
    my_owner = my_pairs // exp_count
    order = jnp.arange(pair_count)
    before = order[:, None] > order[None, :]
    my_slot = jnp.sum((my_owner[:, None] == my_owner[None, :]) & before, axis=1)
    far = jnp.array([d for c in chunks for d in c], jnp.int32) ^ me
    chosen = (
        (my_owner[None, None, :] == far[:, None, None])
        & (my_slot[None, None, :] == jnp.arange(CAP)[None, :, None])
    ).astype(F32)
    by_request = chosen.reshape(groups * CAP, req_count, top_count)
    mask = jnp.repeat(jnp.sum(by_request, axis=2).T, rank, axis=1)
    weight = jnp.repeat(jnp.sum(by_request * router_weights[None], axis=2).T, rank, axis=1)

    rows = len(chunks[0]) * both
    x_spec = pl.BlockSpec((tokens, tile), lambda i: (0, jnp.minimum(i, in_tiles - 1)))
    g_spec = pl.BlockSpec((tokens, tile), lambda i: (0, jnp.maximum(i - in_tiles, 0)))
    piece_spec = pl.BlockSpec((both, tile), lambda i: (0, i))
    small = pl.BlockSpec((req_count, rows), lambda i: (0, 0))
    sums_spec = pl.BlockSpec((2, length, rows), lambda i: (0, 0, 0))
    weighted_spec = pl.BlockSpec((tokens, rows), lambda i: (0, 0))

    back, weighted, sums = {}, [], []
    for n, chunk in enumerate(chunks):
        count = len(chunk)
        my_mask = mask[:, n * rows : (n + 1) * rows]
        if n:
            my_mask, weighted[-1] = lax.optimization_barrier((my_mask, weighted[-1]))
        part = pl.pallas_call(
            functools.partial(project_kernel, count, in_tiles, tiles),
            out_shape=jax.ShapeDtypeStruct((2, length, rows), F32),
            grid=(tiles,),
            in_specs=[small, x_spec, g_spec] + [piece_spec] * count,
            out_specs=sums_spec,
            scratch_shapes=[pltpu.VMEM((rows, tile), BF), pltpu.VMEM((2, tokens, rows), F32)],
        )(my_mask, activations, cotangent, *[got[d] for d in chunk])
        step = 1
        while step < dp:
            part = part + swap(part, "dp", dp, step)
            step *= 2
        done = pl.pallas_call(
            functools.partial(term_kernel, count, in_tiles),
            out_shape=[piece] * count + [jax.ShapeDtypeStruct((tokens, rows), BF)],
            grid=(tiles,),
            in_specs=[sums_spec, small, x_spec, g_spec],
            out_specs=[piece_spec] * count + [weighted_spec],
            scratch_shapes=[pltpu.VMEM((rows, tokens), BF)] * 2,
        )(part, weight[:, n * rows : (n + 1) * rows], activations, cotangent)
        sums.append(part)
        weighted.append(done[-1])
        for d in homes[n]:
            mine = done[chunk.index(d)]
            back[d] = mine if d == 0 else swap(mine, "adapter", groups, d)

    everything = [d for c in chunks for d in c]
    input_grad = pl.pallas_call(
        functools.partial(input_kernel, len(chunks), groups),
        out_shape=jax.ShapeDtypeStruct((tokens, wide), F32),
        grid=(in_tiles,),
        in_specs=[weighted_spec] * len(chunks) + [piece_spec] * groups,
        out_specs=pl.BlockSpec((tokens, tile), lambda i: (0, i)),
        scratch_shapes=[
            pltpu.VMEM((groups * both, tile), BF),
            pltpu.VMEM((tokens, len(chunks) * rows), BF),
        ],
        name="input",
    )(*weighted, *[got[d] for d in everything])

    per_slot = jnp.concatenate([jnp.sum(s[0] * s[1], axis=0) for s in sums])
    per_slot = jnp.sum(per_slot.reshape(groups * CAP, rank), axis=1)
    router_grad = jnp.sum(by_request * per_slot[:, None, None], axis=0)

    stages = [homes[0], homes[1][:-1], homes[1][-1:]]
    tables = [jnp.concatenate([slot_table[d] for d in stage]) for stage in stages]
    early = len(stages[0]) * CAP
    block = math.gcd(exp_count, 4)
    grads = pl.pallas_call(
        functools.partial(collect_kernel, early),
        out_shape=[
            jax.ShapeDtypeStruct(factor_in.shape, BF),
            jax.ShapeDtypeStruct(factor_out.shape, BF),
        ],
        grid=(exp_count // block,),
        in_specs=[SMEM] + [VMEM] * len(stages[0]),
        out_specs=[
            pl.BlockSpec((block, rank, wide), lambda i: (i, 0, 0)),
            pl.BlockSpec((block, rank, narrow), lambda i: (i, 0, 0)),
        ],
        scratch_shapes=[pltpu.VMEM((rank, full), F32)],
        name="collect",
    )(tables[0], *[back[d] for d in stages[0]])
    late, ends = len(stages[1]) * CAP, len(stages[2]) * CAP
    arrays = len(stages[0]) + len(stages[1])
    *grads, ahead = pl.pallas_call(
        functools.partial(finish_kernel, late, early, ends),
        out_shape=[jax.ShapeDtypeStruct(g.shape, BF) for g in grads]
        + [pltpu.VMEM((ends, rank, full), F32)],
        in_specs=[SMEM] * 3 + [VMEM] * len(stages[1]) + [ANY] * len(stages[0]) + [HBM] * 2,
        out_specs=[HBM] * 2 + [VMEM],
        scratch_shapes=[
            pltpu.VMEM((early, rank, full), BF),
            pltpu.VMEM((late, rank, full), BF),
            pltpu.VMEM((rank, full), F32),
            pltpu.SemaphoreType.DMA((early,)),
            pltpu.SemaphoreType.DMA((late, 2)),
        ],
        input_output_aliases={arrays + 3: 0, arrays + 4: 1},
        name="finish1",
    )(tables[1], tables[0], tables[2], *[back[d] for d in stages[1] + stages[0]], *grads)
    on_chip = [pltpu.with_memory_space_constraint(back[d], pltpu.VMEM) for d in stages[2]]
    grads = pl.pallas_call(
        functools.partial(end_kernel, ends),
        out_shape=[jax.ShapeDtypeStruct(g.shape, BF) for g in grads],
        in_specs=[SMEM] + [VMEM] * (len(stages[2]) + 1) + [HBM] * 2,
        out_specs=[HBM] * 2,
        scratch_shapes=[
            pltpu.VMEM((ends, rank, full), BF),
            pltpu.SemaphoreType.DMA((ends, 2)),
        ],
        input_output_aliases={len(stages[2]) + 2: 0, len(stages[2]) + 3: 1},
        name="finish2",
    )(tables[2], *on_chip, pltpu.with_memory_space_constraint(ahead, pltpu.VMEM), *grads)
    grad_factor_in, grad_factor_out = grads
    return (input_grad, grad_factor_in, grad_factor_out, router_grad)


def solution(mesh):
    return jax.shard_map(
        body,
        mesh=mesh,
        in_specs=(
            P("adapter", "dp"),
            P("adapter", "dp"),
            P("adapter", None, "dp"),
            P("adapter", None, "dp"),
            P("adapter", None),
            P("adapter", None),
        ),
        out_specs=(
            P("adapter", "dp"),
            P("adapter", None, "dp"),
            P("adapter", None, "dp"),
            P("adapter", None),
        ),
        check_vma=False,
    )
```

```python
import functools
import math

import jax
import jax.numpy as jnp
from jax import lax
from jax.experimental import pallas as pl
from jax.experimental.pallas import tpu as pltpu
from jax.sharding import PartitionSpec as P


CAP = 2
BF = jnp.bfloat16
F32 = jnp.float32
ANY = pl.BlockSpec(memory_space=pl.ANY)
SMEM = pl.BlockSpec(memory_space=pltpu.SMEM)
VMEM = pl.BlockSpec(memory_space=pltpu.VMEM)
HBM = pl.BlockSpec(memory_space=pltpu.HBM)


def plan(groups):
    steps = [groups >> (i + 1) for i in range(groups.bit_length() - 1)]
    half, last = groups // 2, steps[-1]
    if groups > 4:
        steps[0] += half // 2
    out = []
    for part in (0, last):
        near = [d for d in range(half) if d & last == part]
        far = [d for d in range(half, groups) if d & last == part]
        out.append(near + far)
    home = [list(part) for part in out]
    return steps, out, home


def swap(x, axis, count, offset):
    return lax.ppermute(x, axis, [(i, i ^ offset) for i in range(count)])


def pick_kernel(groups, ids_ref, fin, fout, table_ref, *refs):
    outs = refs[:groups]
    in_sem, ids, ids_sem = refs[groups:]
    fetch = pltpu.make_async_copy(ids_ref, ids, ids_sem)
    fetch.start()
    fetch.wait()
    exp_count, rank, wide = fin.shape
    base = lax.axis_index("adapter") * exp_count
    loads = []
    for m in range(groups):
        found = jnp.int32(0)
        picks = [jnp.int32(-1)] * CAP
        for b in range(ids_ref.shape[1]):
            for k in range(ids_ref.shape[2]):
                local = ids[m, b, k] - base
                mine = (local >= 0) & (local < exp_count)
                for c in range(CAP):
                    picks[c] = jnp.where(mine & (found == c), local, picks[c])
                found = found + mine.astype(jnp.int32)
        for c in range(CAP):
            table_ref[m, c] = picks[c]
            e = jnp.maximum(picks[c], 0)
            rows = pl.ds(c * rank, rank)
            one = pltpu.make_async_copy(
                fin.at[e], outs[m].at[rows, pl.ds(0, wide)], in_sem.at[m, c, 0]
            )
            two = pltpu.make_async_copy(
                fout.at[e], outs[m].at[rows, pl.ds(wide, fout.shape[2])], in_sem.at[m, c, 1]
            )
            one.start()
            two.start()
            loads.append((one, two))
    for pair in loads:
        for load in pair:
            load.wait()


def project_kernel(groups, in_tiles, tiles, mask_ref, x_ref, g_ref, *refs):
    pieces = refs[:groups]
    out_ref, rows, total = refs[groups:]
    i = pl.program_id(0)
    rank = pieces[0].shape[0]
    for d in range(groups):
        rows[pl.ds(d * rank, rank), :] = pieces[d][...]
    dims = (((1,), (1,)), ((), ()))

    def add(side, data_ref, first):
        part = lax.dot_general(data_ref[...], rows[...], dims, preferred_element_type=F32)

        @pl.when(first)
        def _():
            total[side] = part

        @pl.when(jnp.logical_not(first))
        def _():
            total[side] += part

    @pl.when(i < in_tiles)
    def _():
        add(0, x_ref, i == 0)

    @pl.when(i >= in_tiles)
    def _():
        add(1, g_ref, i == in_tiles)

    @pl.when(i == tiles - 1)
    def _():
        length = out_ref.shape[1]
        for side in range(2):
            acc = jnp.zeros(out_ref.shape[1:], F32)
            for b in range(mask_ref.shape[0]):
                part = total[side, pl.ds(b * length, length), :]
                acc = jnp.where(mask_ref[b : b + 1, :] > 0, part, acc)
            out_ref[side] = acc


def term_kernel(groups, in_tiles, sums_ref, weight_ref, x_ref, g_ref, *refs):
    outs = refs[:groups]
    weighted_ref, pulled, projected = refs[groups:]
    i = pl.program_id(0)
    rank = outs[0].shape[0]

    @pl.when(i == 0)
    def _():
        length = sums_ref.shape[1]
        for b in range(weight_ref.shape[0]):
            w = weight_ref[b : b + 1, :]
            span = pl.ds(b * length, length)
            part = sums_ref[1] * w
            weighted_ref[span, :] = part.astype(BF)
            pulled[:, span] = part.T.astype(BF)
            projected[:, span] = (sums_ref[0] * w).T.astype(BF)

    @pl.when(i < in_tiles)
    def _():
        part = jnp.dot(pulled[...], x_ref[...], preferred_element_type=F32).astype(BF)
        for d in range(groups):
            outs[d][...] = part[d * rank : (d + 1) * rank]

    @pl.when(i >= in_tiles)
    def _():
        part = jnp.dot(projected[...], g_ref[...], preferred_element_type=F32).astype(BF)
        for d in range(groups):
            outs[d][...] = part[d * rank : (d + 1) * rank]


def input_kernel(chunks, count, *refs):
    weighted = refs[:chunks]
    pieces = refs[chunks : chunks + count]
    out_ref, rows, left = refs[chunks + count :]
    rank = pieces[0].shape[0]
    half = weighted[0].shape[1]

    @pl.when(pl.program_id(0) == 0)
    def _():
        for c in range(chunks):
            left[:, pl.ds(c * half, half)] = weighted[c][...]

    for m in range(count):
        rows[pl.ds(m * rank, rank), :] = pieces[m][...]
    out_ref[...] = jnp.dot(left[...], rows[...], preferred_element_type=F32)


def place(refs, m, rank):
    return refs[m // CAP].at[pl.ds((m % CAP) * rank, rank), :]


def collect_kernel(count, table_ref, *refs):
    pieces = refs[: count // CAP]
    in_ref, out_ref, total = refs[count // CAP :]
    block, rank, wide = in_ref.shape
    for s in range(block):
        e = pl.program_id(0) * block + s
        total[...] = jnp.zeros_like(total)
        for m in range(count):

            @pl.when(table_ref[m] == e)
            def _():
                total[...] += place(pieces, m, rank)[...].astype(F32)

        in_ref[s] = total[:, :wide].astype(BF)
        out_ref[s] = total[:, wide:].astype(BF)


def fresh(table_ref, s):
    new = table_ref[s] >= 0
    for r in range(s):
        new = new & (table_ref[r] != table_ref[s])
    return new


def stores(table_ref, s, stage, in_hbm, out_hbm, out_sem):
    e = jnp.maximum(table_ref[s], 0)
    wide, narrow = in_hbm.shape[2], out_hbm.shape[2]
    return (
        pltpu.make_async_copy(stage.at[s, :, pl.ds(0, wide)], in_hbm.at[e], out_sem.at[s, 0]),
        pltpu.make_async_copy(stage.at[s, :, pl.ds(wide, narrow)], out_hbm.at[e], out_sem.at[s, 1]),
    )


def finish_kernel(late, early, ends, late_ref, early_ref, end_ref, *refs):
    a, b = late // CAP, early // CAP
    late_refs, early_hbm = refs[:a], refs[a : a + b]
    in_hbm, out_hbm, ahead, kept, stage, total, kept_sem, out_sem = refs[a + b + 2 :]
    rank, _ = total.shape

    def load_early(m):
        return pltpu.make_async_copy(place(early_hbm, m, rank), kept.at[m], kept_sem.at[m])

    def used(m):
        hit = late_ref[0] == early_ref[m]
        for s in range(1, late):
            hit = hit | (late_ref[s] == early_ref[m])
        for s in range(ends):
            hit = hit | (end_ref[s] == early_ref[m])
        return hit & (early_ref[m] >= 0)

    def add(e, known, known_ref, terms):
        for m in range(known):

            @pl.when((known_ref[m] == e) & (e >= 0))
            def _():
                total[...] += terms(m)[...].astype(F32)

    for m in range(early):

        @pl.when(used(m))
        def _():
            load_early(m).start()

    for m in range(early):

        @pl.when(used(m))
        def _():
            load_early(m).wait()

    for s in range(late):

        @pl.when(fresh(late_ref, s))
        def _():
            total[...] = jnp.zeros_like(total)
            add(late_ref[s], late, late_ref, lambda m: place(late_refs, m, rank))
            add(late_ref[s], early, early_ref, lambda m: kept.at[m])
            stage[s] = total[...].astype(BF)
            for store in stores(late_ref, s, stage, in_hbm, out_hbm, out_sem):
                store.start()

    for s in range(ends):
        total[...] = jnp.zeros_like(total)
        add(end_ref[s], late, late_ref, lambda m: place(late_refs, m, rank))
        add(end_ref[s], early, early_ref, lambda m: kept.at[m])
        ahead[s] = total[...]

    for s in range(late):

        @pl.when(fresh(late_ref, s))
        def _():
            for store in stores(late_ref, s, stage, in_hbm, out_hbm, out_sem):
                store.wait()


def end_kernel(ends, end_ref, *refs):
    end_refs, ahead = refs[: ends // CAP], refs[ends // CAP]
    in_hbm, out_hbm, stage, out_sem = refs[ends // CAP + 3 :]
    rank = stage.shape[1]
    for s in range(ends):

        @pl.when(fresh(end_ref, s))
        def _():
            stage[s] = (place(end_refs, s, rank)[...].astype(F32) + ahead[s]).astype(BF)
            for r in range(s + 1, ends):

                @pl.when(end_ref[r] == end_ref[s])
                def _():
                    total = ahead[s]
                    for m in range(s, ends):
                        same = (end_ref[m] == end_ref[s]).astype(F32)
                        total = total + same * place(end_refs, m, rank)[...].astype(F32)
                    stage[s] = total.astype(BF)

            for store in stores(end_ref, s, stage, in_hbm, out_hbm, out_sem):
                store.start()

    for s in range(ends):

        @pl.when(fresh(end_ref, s))
        def _():
            for store in stores(end_ref, s, stage, in_hbm, out_hbm, out_sem):
                store.wait()


def body(activations, cotangent, factor_in, factor_out, adapter_ids, router_weights):
    groups = lax.axis_size("adapter")
    dp = lax.axis_size("dp")
    me = lax.axis_index("adapter")
    exp_count, rank, wide = factor_in.shape
    narrow = factor_out.shape[2]
    req_count, top_count = adapter_ids.shape
    pair_count = req_count * top_count
    tokens = activations.shape[0]
    length = tokens // req_count
    full = wide + narrow
    tile = math.gcd(wide, narrow)
    in_tiles, tiles = wide // tile, full // tile
    both = CAP * rank
    piece = jax.ShapeDtypeStruct((both, full), BF)

    def pick(lists, fast):
        count = lists.shape[0]
        return pl.pallas_call(
            functools.partial(pick_kernel, count),
            out_shape=[jax.ShapeDtypeStruct((count, CAP), jnp.int32)]
            + [pltpu.VMEM((both, full), BF) if fast else piece] * count,
            in_specs=[VMEM, HBM, HBM],
            out_specs=[SMEM] + [VMEM] * count,
            scratch_shapes=[
                pltpu.SemaphoreType.DMA((count, CAP, 2)),
                pltpu.SMEM(lists.shape, jnp.int32),
                pltpu.SemaphoreType.DMA,
            ],
        )(pltpu.with_memory_space_constraint(lists, pltpu.VMEM), factor_in, factor_out)

    steps, chunks, homes = plan(groups)
    lists, known = adapter_ids[None], [0]
    slot_table, sent, got = {}, {}, {}
    arrivals = []
    for step in steps:
        fresh = swap(lists, "adapter", groups, step)
        arrivals.append(([d ^ step for d in known], fresh))
        lists = jnp.concatenate([lists, fresh], axis=0)
        known = known + [d ^ step for d in known]
    arrivals.append(([0], adapter_ids[None]))
    for n, (which, fresh) in enumerate(arrivals):
        picked = pick(fresh, n == 0)
        for m, d in enumerate(which):
            slot_table[d] = picked[0][m]
            sent[d] = picked[1 + m]
    for chunk in chunks:
        for d in chunk:
            got[d] = sent[d] if d == 0 else swap(sent[d], "adapter", groups, d)

    my_pairs = adapter_ids.reshape(pair_count)
    my_owner = my_pairs // exp_count
    order = jnp.arange(pair_count)
    before = order[:, None] > order[None, :]
    my_slot = jnp.sum((my_owner[:, None] == my_owner[None, :]) & before, axis=1)
    far = jnp.array([d for c in chunks for d in c], jnp.int32) ^ me
    chosen = (
        (my_owner[None, None, :] == far[:, None, None])
        & (my_slot[None, None, :] == jnp.arange(CAP)[None, :, None])
    ).astype(F32)
    by_request = chosen.reshape(groups * CAP, req_count, top_count)
    mask = jnp.repeat(jnp.sum(by_request, axis=2).T, rank, axis=1)
    weight = jnp.repeat(jnp.sum(by_request * router_weights[None], axis=2).T, rank, axis=1)

    rows = len(chunks[0]) * both
    x_spec = pl.BlockSpec((tokens, tile), lambda i: (0, jnp.minimum(i, in_tiles - 1)))
    g_spec = pl.BlockSpec((tokens, tile), lambda i: (0, jnp.maximum(i - in_tiles, 0)))
    piece_spec = pl.BlockSpec((both, tile), lambda i: (0, i))
    small = pl.BlockSpec((req_count, rows), lambda i: (0, 0))
    sums_spec = pl.BlockSpec((2, length, rows), lambda i: (0, 0, 0))
    weighted_spec = pl.BlockSpec((tokens, rows), lambda i: (0, 0))

    back, weighted, sums = {}, [], []
    for n, chunk in enumerate(chunks):
        count = len(chunk)
        my_mask = mask[:, n * rows : (n + 1) * rows]
        if n:
            my_mask, weighted[-1] = lax.optimization_barrier((my_mask, weighted[-1]))
        part = pl.pallas_call(
            functools.partial(project_kernel, count, in_tiles, tiles),
            out_shape=jax.ShapeDtypeStruct((2, length, rows), F32),
            grid=(tiles,),
            in_specs=[small, x_spec, g_spec] + [piece_spec] * count,
            out_specs=sums_spec,
            scratch_shapes=[pltpu.VMEM((rows, tile), BF), pltpu.VMEM((2, tokens, rows), F32)],
        )(my_mask, activations, cotangent, *[got[d] for d in chunk])
        step = 1
        while step < dp:
            part = part + swap(part, "dp", dp, step)
            step *= 2
        done = pl.pallas_call(
            functools.partial(term_kernel, count, in_tiles),
            out_shape=[piece] * count + [jax.ShapeDtypeStruct((tokens, rows), BF)],
            grid=(tiles,),
            in_specs=[sums_spec, small, x_spec, g_spec],
            out_specs=[piece_spec] * count + [weighted_spec],
            scratch_shapes=[pltpu.VMEM((rows, tokens), BF)] * 2,
        )(part, weight[:, n * rows : (n + 1) * rows], activations, cotangent)
        sums.append(part)
        weighted.append(done[-1])
        for d in homes[n]:
            mine = done[chunk.index(d)]
            back[d] = mine if d == 0 else swap(mine, "adapter", groups, d)

    everything = [d for c in chunks for d in c]
    input_grad = pl.pallas_call(
        functools.partial(input_kernel, len(chunks), groups),
        out_shape=jax.ShapeDtypeStruct((tokens, wide), F32),
        grid=(in_tiles,),
        in_specs=[weighted_spec] * len(chunks) + [piece_spec] * groups,
        out_specs=pl.BlockSpec((tokens, tile), lambda i: (0, i)),
        scratch_shapes=[
            pltpu.VMEM((groups * both, tile), BF),
            pltpu.VMEM((tokens, len(chunks) * rows), BF),
        ],
        name="input",
    )(*weighted, *[got[d] for d in everything])

    per_slot = jnp.concatenate([jnp.sum(s[0] * s[1], axis=0) for s in sums])
    per_slot = jnp.sum(per_slot.reshape(groups * CAP, rank), axis=1)
    router_grad = jnp.sum(by_request * per_slot[:, None, None], axis=0)

    stages = [homes[0], homes[1][:-1], homes[1][-1:]]
    tables = [jnp.concatenate([slot_table[d] for d in stage]) for stage in stages]
    early = len(stages[0]) * CAP
    block = math.gcd(exp_count, 4)
    grads = pl.pallas_call(
        functools.partial(collect_kernel, early),
        out_shape=[
            jax.ShapeDtypeStruct(factor_in.shape, BF),
            jax.ShapeDtypeStruct(factor_out.shape, BF),
        ],
        grid=(exp_count // block,),
        in_specs=[SMEM] + [VMEM] * len(stages[0]),
        out_specs=[
            pl.BlockSpec((block, rank, wide), lambda i: (i, 0, 0)),
            pl.BlockSpec((block, rank, narrow), lambda i: (i, 0, 0)),
        ],
        scratch_shapes=[pltpu.VMEM((rank, full), F32)],
        name="collect",
    )(tables[0], *[back[d] for d in stages[0]])
    late, ends = len(stages[1]) * CAP, len(stages[2]) * CAP
    arrays = len(stages[0]) + len(stages[1])
    *grads, ahead = pl.pallas_call(
        functools.partial(finish_kernel, late, early, ends),
        out_shape=[jax.ShapeDtypeStruct(g.shape, BF) for g in grads]
        + [pltpu.VMEM((ends, rank, full), F32)],
        in_specs=[SMEM] * 3 + [VMEM] * len(stages[1]) + [ANY] * len(stages[0]) + [HBM] * 2,
        out_specs=[HBM] * 2 + [VMEM],
        scratch_shapes=[
            pltpu.VMEM((early, rank, full), BF),
            pltpu.VMEM((late, rank, full), BF),
            pltpu.VMEM((rank, full), F32),
            pltpu.SemaphoreType.DMA((early,)),
            pltpu.SemaphoreType.DMA((late, 2)),
        ],
        input_output_aliases={arrays + 3: 0, arrays + 4: 1},
        name="finish1",
    )(tables[1], tables[0], tables[2], *[back[d] for d in stages[1] + stages[0]], *grads)
    on_chip = [pltpu.with_memory_space_constraint(back[d], pltpu.VMEM) for d in stages[2]]
    grads = pl.pallas_call(
        functools.partial(end_kernel, ends),
        out_shape=[jax.ShapeDtypeStruct(g.shape, BF) for g in grads],
        in_specs=[SMEM] + [VMEM] * (len(stages[2]) + 1) + [HBM] * 2,
        out_specs=[HBM] * 2,
        scratch_shapes=[
            pltpu.VMEM((ends, rank, full), BF),
            pltpu.SemaphoreType.DMA((ends, 2)),
        ],
        input_output_aliases={len(stages[2]) + 2: 0, len(stages[2]) + 3: 1},
        name="finish2",
    )(tables[2], *on_chip, pltpu.with_memory_space_constraint(ahead, pltpu.VMEM), *grads)
    grad_factor_in, grad_factor_out = grads
    return (input_grad, grad_factor_in, grad_factor_out, router_grad)


def solution(mesh):
    return jax.shard_map(
        body,
        mesh=mesh,
        in_specs=(
            P("adapter", "dp"),
            P("adapter", "dp"),
            P("adapter", None, "dp"),
            P("adapter", None, "dp"),
            P("adapter", None),
            P("adapter", None),
        ),
        out_specs=(
            P("adapter", "dp"),
            P("adapter", None, "dp"),
            P("adapter", None, "dp"),
            P("adapter", None),
        ),
        check_vma=False,
    )
```
